32 devices in a mesh: cell: 2 (over y), gene: 16 (over z, x, core).
Axes of the slice: x: 2, y: 2, z: 4, core: 2. Of those that a mesh axis runs over, the one named last changes fastest.
Arguments:
- blocks: bfloat16 [1536, 256, 256], P(('cell', 'gene')), may hold values from 0 to 255, as said below
- block_rows: int32 [1536], P(('cell', 'gene')), may hold values from 0 to 15, as said below
- block_cols: int32 [1536], P(('cell', 'gene')), may hold values from 0 to 3, as said below
- block_count: int32 [32], P(('cell', 'gene')), may hold values from 2 to 48, as said below
- cell_factor: float32 [8192, 128], P(('cell', 'gene')), as said below
- gene_factor: float32 [16384, 128], P('gene'), as said below
Outputs:
- cell_new: float32 [8192, 128], P(('cell', 'gene'))
- gene_new: float32 [16384, 128], P('gene')
The draws below stay inside these ranges and needn't reach their ends.
Inputs may be any that keep to these rules, and one draw needn't show every extreme that they name: `blocks`: counts are whole numbers. `block_rows`: within one device the live slots and the padding slots name distinct block positions. `block_cols`: within one device the live slots and the padding slots name distinct block positions. `block_count`: some device has all 48 slots live. `cell_factor`: positive entries. `gene_factor`: positive entries.
All inputs are finite; a program needn't handle non-finite values.
Results may differ from the reference program's by a relative error of at most 0.00084.
Values may be sent and summed in bfloat16 or wider, within the bound.
A program may use at most 64 MiB of HBM per device.

```python
import jax
import jax.numpy as jnp
from jax import lax

BLK = 256
R = 128
GENE_DEV = 1024
CELL_DEV = 4096
NB_DEV = 48
CELLS = 8192
GENES = 16384
N_CELL = 2
N_GENE = 16


def positions(key):
    devs = N_CELL * N_GENE
    keys = jax.random.split(jax.random.fold_in(key, 7), devs)
    total = CELL_DEV // BLK * (GENE_DEV // BLK)
    picked = jax.vmap(lambda one: jax.random.permutation(one, total)[:NB_DEV])(keys)
    return picked.reshape(-1).astype(jnp.int32)


def draw_block_rows(key, part):
    return (positions(key) // (GENE_DEV // BLK)).astype(jnp.int32)


def draw_block_cols(key, part):
    return (positions(key) % (GENE_DEV // BLK)).astype(jnp.int32)


def draw_block_count(key, part):
    devs = N_CELL * N_GENE
    first_key = jax.random.fold_in(key, 21)
    second_key = jax.random.fold_in(key, 22)
    third_key = jax.random.fold_in(key, 23)
    left = jax.random.randint(first_key, (devs,), 0, NB_DEV - 1)
    right = jax.random.randint(second_key, (devs,), 0, NB_DEV - 1)
    counts = 2 + left * right // (NB_DEV - 2)
    fullest = jax.random.randint(third_key, (), 0, devs)
    return jnp.where(jnp.arange(devs) == fullest, NB_DEV, counts).astype(jnp.int32)


def draw_blocks(key, part):
    shape = (N_CELL * N_GENE * NB_DEV, BLK, BLK)
    inner = jax.random.fold_in(key, 3)
    values = jax.random.randint(inner, shape, 0, 256)
    return values.astype(jnp.float32).astype(jnp.bfloat16)


def factor_draw(key, count):
    base_key = jax.random.fold_in(key, 41)
    rank_key = jax.random.fold_in(key, 42)
    boost_key = jax.random.fold_in(key, 43)
    rising = 1.0 + 2.0 * jnp.arange(count, dtype=jnp.float32)[:, None] / count
    leading = max(1, R // 32)
    chosen_ranks = jax.random.randint(rank_key, (count, leading), 0, R)
    ranks = jnp.arange(R, dtype=jnp.int32)[None, :]
    marked = jnp.zeros((count, R), jnp.float32)
    for which in range(leading):
        marked = jnp.maximum(marked, (chosen_ranks[:, which:which + 1] == ranks).astype(jnp.float32))
    base = jnp.exp(jax.random.uniform(base_key, (count, R), jnp.float32, jnp.log(0.05), jnp.log(0.5)))
    boost = jnp.exp(jax.random.uniform(boost_key, (count, R), jnp.float32, jnp.log(3.0), jnp.log(12.0)))
    entries = jnp.where(marked > 0.0, boost, base)
    return (entries * rising).astype(jnp.float32)


def draw_cell_factor(key, part):
    return factor_draw(jax.random.fold_in(key, 51), CELLS)


def draw_gene_factor(key, part):
    return factor_draw(jax.random.fold_in(key, 52), GENES)


def setup_inputs(seed: int = 0) -> dict:
    arg_keys = jax.random.split(jax.random.key(seed), 7)
    blocks = draw_blocks(jax.random.fold_in(arg_keys[6], 71), 0)
    block_rows = draw_block_rows(jax.random.fold_in(arg_keys[6], 71), 0)
    block_cols = draw_block_cols(jax.random.fold_in(arg_keys[6], 71), 0)
    block_count = draw_block_count(jax.random.fold_in(arg_keys[6], 71), 0)
    cell_factor = draw_cell_factor(jax.random.fold_in(arg_keys[6], 71), 0)
    gene_factor = draw_gene_factor(jax.random.fold_in(arg_keys[6], 71), 0)
    return dict(blocks=blocks, block_rows=block_rows, block_cols=block_cols, block_count=block_count, cell_factor=cell_factor, gene_factor=gene_factor)


def block_ratio(tiles, row_tiles, col_tiles, live):
    model = jnp.einsum('nir,njr->nij', row_tiles.astype(jnp.float32), col_tiles.astype(jnp.float32))
    return (tiles.astype(jnp.float32) / model * live[:, None, None]).astype(jnp.bfloat16)


def reference(blocks, block_rows, block_cols, block_count, cell_factor, gene_factor):
    devs = N_CELL * N_GENE
    row_blocks = CELL_DEV // BLK
    col_blocks = GENE_DEV // BLK
    tiles = blocks.reshape(devs, NB_DEV, BLK, BLK)
    rows = block_rows.reshape(devs, NB_DEV).astype(jnp.int32)
    cols = block_cols.reshape(devs, NB_DEV).astype(jnp.int32)
    counts = block_count.astype(jnp.int32)
    order = jnp.arange(devs, dtype=jnp.int32)
    cell_bf = cell_factor.astype(jnp.bfloat16)
    gene_bf = gene_factor.astype(jnp.bfloat16)

    def prepare(cell_src, item):
        tile, row, col, count, index = item
        cstart = ((index // N_GENE) * CELL_DEV).astype(jnp.int32)
        gstart = ((index % N_GENE) * GENE_DEV).astype(jnp.int32)
        w_tile = lax.dynamic_slice_in_dim(cell_src, cstart, CELL_DEV, 0)
        h_tile = lax.dynamic_slice_in_dim(gene_bf, gstart, GENE_DEV, 0)
        live = (jnp.arange(NB_DEV, dtype=jnp.int32) < count).astype(jnp.float32)
        row_tiles = w_tile.reshape(row_blocks, BLK, R)[row]
        col_tiles = h_tile.reshape(col_blocks, BLK, R)[col]
        ratio = block_ratio(tile, row_tiles, col_tiles, live)
        return ratio, row_tiles, col_tiles, cstart, gstart

    def first(carry, item):
        ratio, row_tiles, col_tiles, cstart, gstart = prepare(cell_bf, item)
        terms = jnp.einsum('nij,njr->nir', ratio.astype(jnp.float32), col_tiles.astype(jnp.float32))
        sums = jax.ops.segment_sum(terms, item[1], num_segments=row_blocks).reshape(CELL_DEV, R)
        old = lax.dynamic_slice_in_dim(carry, cstart, CELL_DEV, 0)
        return lax.dynamic_update_slice_in_dim(carry, old + sums, cstart, 0), None

    numer_w, unused = lax.scan(first, jnp.zeros((CELLS, R), jnp.float32), (tiles, rows, cols, counts, order))
    gene_sums = jnp.sum(gene_factor, 0)
    cell_new = cell_factor * numer_w / gene_sums
    new_bf = cell_new.astype(jnp.bfloat16)

    def second(carry, item):
        ratio, row_tiles, col_tiles, cstart, gstart = prepare(new_bf, item)
        terms = jnp.einsum('nij,nir->njr', ratio.astype(jnp.float32), row_tiles.astype(jnp.float32))
        sums = jax.ops.segment_sum(terms, item[2], num_segments=col_blocks).reshape(GENE_DEV, R)
        old = lax.dynamic_slice_in_dim(carry, gstart, GENE_DEV, 0)
        return lax.dynamic_update_slice_in_dim(carry, old + sums, gstart, 0), None

    numer_h, unused = lax.scan(second, jnp.zeros((GENES, R), jnp.float32), (tiles, rows, cols, counts, order))
    cell_sums = jnp.sum(cell_new, 0)
    gene_new = gene_factor * numer_h / cell_sums
    return cell_new, gene_new
```

```python
import functools

import jax
import jax.numpy as jnp
from jax import lax
from jax.experimental import pallas as pl
from jax.experimental.pallas import tpu as pltpu
from jax.sharding import PartitionSpec as P

MESH = pl.DeviceIdType.MESH
F32 = jnp.float32
BF = jnp.bfloat16


def digits(group):
    cores = 2
    far = 4
    return far, group // (far * cores), cores


class Spot:
    def __init__(self, group):
        self.group = group
        self.far, self.near, self.cores = digits(group)
        self.me = lax.axis_index("gene")
        self.a = self.me // (self.near * self.cores)
        self.b = lax.rem(self.me // self.cores, self.near)
        self.c = lax.rem(self.me, self.cores)

    def a_at(self, d):
        return lax.rem(self.a + d, self.far)

    def b_at(self, d):
        return lax.rem(self.b + d, self.near)

    def index(self, a, b, c):
        return (a * self.near + b) * self.cores + c


def send(src, dst, send_sem, recv_sem, where):
    copy = pltpu.make_async_remote_copy(
        src_ref=src, dst_ref=dst, send_sem=send_sem, recv_sem=recv_sem,
        device_id=where, device_id_type=MESH,
    )
    copy.start()
    return copy


def greet_group(spot):
    barrier = pltpu.get_barrier_semaphore()
    for d in range(1, spot.group):
        pl.semaphore_signal(
            barrier, inc=1, device_id={"gene": lax.rem(spot.me + d, spot.group)}, device_id_type=MESH
        )
    pl.semaphore_wait(barrier, spot.group - 1)


def far_order(far):
    order = []
    for step in range(1, far // 2 + 1):
        order.append(step)
        if far - step != step:
            order.append(far - step)
    return order


def gather_chunks(spot, own, out, zs, zr, xs, xr, cs, cr):
    far, near = spot.far, spot.near
    a, b, c = spot.a, spot.b, spot.c
    pending = []
    zc, xc, cc = {}, {}, {}
    for d in far_order(far):
        zc[d] = send(own, out.at[spot.index(a, b, c)], zs.at[d], zr.at[d],
                     {"gene": spot.index(spot.a_at(d), b, c)})

    def forward_x(d, src):
        for e in range(1, near):
            xc[d, e] = send(src, out.at[spot.index(spot.a_at(far - d), b, c)],
                            xs.at[d, e], xr.at[d, e], {"gene": spot.index(a, spot.b_at(e), c)})

    def forward_c(d, e, src):
        at = spot.index(spot.a_at(far - d), spot.b_at(near - e), c)
        cc[d, e] = send(src, out.at[at], cs.at[d, e], cr.at[d, e],
                        {"gene": spot.index(a, b, 1 - c)})

    forward_x(0, own)
    forward_c(0, 0, own)
    order = [0] + far_order(far)
    for i, d in enumerate(order):
        if d:
            zc[d].wait_recv()
            src = out.at[spot.index(spot.a_at(far - d), b, c)]
            forward_x(d, src)
            forward_c(d, 0, src)
        if i:
            arrive_x(spot, order[i - 1], xc, forward_c, out)
    arrive_x(spot, order[-1], xc, forward_c, out)
    for copy in cc.values():
        copy.wait_recv()
    for copy in [*zc.values(), *xc.values(), *cc.values()]:
        copy.wait_send()


def arrive_x(spot, d, xc, forward_c, out):
    for e in range(1, spot.near):
        xc[d, e].wait_recv()
        at = spot.index(spot.a_at(spot.far - d), spot.b_at(spot.near - e), spot.c)
        forward_c(d, e, out.at[at])


def share_start(spot, src, parts, ss, sr):
    return [
        send(src, parts.at[spot.me], ss.at[d], sr.at[d], {"gene": lax.rem(spot.me + d, spot.group)})
        for d in range(1, spot.group)
    ]


def gather_kernel(group, own, sums, out, parts, zs, zr, xs, xr, cs, cr, ss, sr, ls):
    spot = Spot(group)
    mine = pltpu.make_async_copy(own, out.at[spot.me], ls.at[0])
    mine_sum = pltpu.make_async_copy(sums, parts.at[spot.me], ls.at[1])
    mine.start()
    mine_sum.start()
    greet_group(spot)
    shared = share_start(spot, sums, parts, ss, sr)
    gather_chunks(spot, own, out, zs, zr, xs, xr, cs, cr)
    for copy in shared:
        copy.wait()
    mine.wait()
    mine_sum.wait()


def gather_sems(group):
    far, near, cores = digits(group)
    dma = pltpu.SemaphoreType.DMA
    return [dma((far,)), dma((far,)), dma((far, near)), dma((far, near)),
            dma((far, near)), dma((far, near)), dma((group,)), dma((group,)), dma((2,))]


VMEM = pl.BlockSpec(memory_space=pltpu.VMEM)
SMEM = pl.BlockSpec(memory_space=pltpu.SMEM)
ANY = pl.BlockSpec(memory_space=pl.ANY)


def gather(group, own, sums):
    return pl.pallas_call(
        functools.partial(gather_kernel, group),
        out_shape=(
            jax.ShapeDtypeStruct((group,) + own.shape, own.dtype),
            jax.ShapeDtypeStruct((group,) + sums.shape, sums.dtype),
        ),
        in_specs=[VMEM, VMEM],
        out_specs=(VMEM, VMEM),
        scratch_shapes=gather_sems(group),
        compiler_params=pltpu.CompilerParams(collective_id=0, has_side_effects=True),
        name="gather_cells",
    )(own, sums)


def update_kernel(group, numer, totals, cell, fresh, out, parts, own_bf, own_sum,
                  p1, p2, p3, t2, t3,
                  zs, zr, xs, xr, cs, cr, ss, sr, ls, s1, r1, s2, r2, s3, r3):
    spot = Spot(group)
    far, near = spot.far, spot.near
    a, b, c = spot.a, spot.b, spot.c
    greet_group(spot)
    c1, c2, c3 = {}, {}, {}
    order = far_order(far) + [0]
    for d in order:
        for e in [*range(1, near), 0]:
            at = spot.index(spot.a_at(d), spot.b_at(e), 1 - c)
            c1[d, e] = send(numer.at[at], p1.at[d, e], s1.at[d, e], r1.at[d, e],
                            {"gene": spot.index(a, b, 1 - c)})

    def stage_two(d):
        for e in range(1, near):
            c1[d, e].wait_recv()
            t2[d, e] = numer[spot.index(spot.a_at(d), spot.b_at(e), c)] + p1[d, e]
            c2[d, e] = send(t2.at[d, e], p2.at[d, e], s2.at[d, e], r2.at[d, e],
                            {"gene": spot.index(a, spot.b_at(e), c)})

    def held(d):
        c1[d, 0].wait_recv()
        value = numer[spot.index(spot.a_at(d), b, c)] + p1[d, 0]
        for e in range(1, near):
            c2[d, e].wait_recv()
            value += p2[d, e]
        return value

    def stage_three(d):
        t3[d] = held(d)
        c3[d] = send(t3.at[d], p3.at[d], s3.at[d], r3.at[d],
                     {"gene": spot.index(spot.a_at(d), b, c)})

    for d in order:
        stage_two(d)
    for d in order[:-1]:
        stage_three(d)
    value = held(0)
    for d in order[:-1]:
        c3[d].wait_recv()
        value += p3[d]
    total = jnp.sum(totals[...], axis=0)
    new = cell[...] * value / total
    fresh[...] = new
    own_bf[...] = new.astype(BF)
    own_sum[...] = jnp.sum(new, axis=0, keepdims=True)
    mine = pltpu.make_async_copy(own_bf, out.at[spot.me], ls.at[0])
    mine_sum = pltpu.make_async_copy(own_sum, parts.at[spot.me], ls.at[1])
    mine.start()
    mine_sum.start()
    shared = share_start(spot, own_sum, parts, ss, sr)
    gather_chunks(spot, own_bf, out, zs, zr, xs, xr, cs, cr)
    for copy in shared:
        copy.wait()
    for copy in [*c1.values(), *c2.values(), *c3.values()]:
        copy.wait_send()
    mine.wait()
    mine_sum.wait()


def update_cells(group, numer, totals, cell):
    far, near, cores = digits(group)
    rows, rank = cell.shape
    dma = pltpu.SemaphoreType.DMA
    return pl.pallas_call(
        functools.partial(update_kernel, group),
        out_shape=(
            jax.ShapeDtypeStruct((rows, rank), F32),
            jax.ShapeDtypeStruct((group, rows, rank), BF),
            jax.ShapeDtypeStruct((group, 1, rank), F32),
        ),
        in_specs=[VMEM] * 3,
        out_specs=(VMEM,) * 3,
        scratch_shapes=[
            pltpu.VMEM((rows, rank), BF),
            pltpu.VMEM((1, rank), F32),
            pltpu.VMEM((far, near, rows, rank), F32),
            pltpu.VMEM((far, near, rows, rank), F32),
            pltpu.VMEM((far, rows, rank), F32),
            pltpu.VMEM((far, near, rows, rank), F32),
            pltpu.VMEM((far, rows, rank), F32),
        ] + gather_sems(group) + [dma((far, near))] * 4 + [dma((far,))] * 2,
        compiler_params=pltpu.CompilerParams(collective_id=1, has_side_effects=True),
        name="update_cells",
    )(numer.reshape(group, rows, rank), totals, cell)


def start_blocks(count, blocks, held, sems):
    @pl.loop(0, count)
    def _(s):
        pltpu.make_async_copy(blocks.at[s], held.at[s], sems.at[s]).start()


def pass_one_kernel(blocks, brow, bcol, bcount, cell, gene, numer, held, flipped, sems):
    count = bcount[0]
    start_blocks(count, blocks, held, sems)
    numer[...] = jnp.zeros_like(numer)
    for j in range(gene.shape[0]):
        flipped[j] = gene[j].T

    @pl.loop(0, count)
    def _(s):
        r, j = brow[s], bcol[s]
        pltpu.make_async_copy(blocks.at[s], held.at[s], sems.at[s]).wait()
        model = jnp.dot(cell[r], flipped[j], preferred_element_type=F32)
        ratio = (held[s].astype(F32) / model).astype(BF)
        numer[r] += jnp.dot(ratio, gene[j], preferred_element_type=F32)


def pass_two_kernel(blocks, brow, bcol, bcount, cell, gene, numer, held, flipped, sems):
    count = bcount[0]
    start_blocks(count, blocks, held, sems)
    numer[...] = jnp.zeros_like(numer)
    for j in range(gene.shape[0]):
        flipped[j] = gene[j].T

    @pl.loop(0, count)
    def _(s):
        r, j = brow[s], bcol[s]
        pltpu.make_async_copy(blocks.at[s], held.at[s], sems.at[s]).wait()
        rows = cell[r]
        model = jnp.dot(rows, flipped[j], preferred_element_type=F32)
        ratio = (held[s].astype(F32) / model).astype(BF)
        numer[j] += lax.dot_general(
            ratio, rows, (((0,), (0,)), ((), ())), preferred_element_type=F32
        )


def block_pass(kernel, name, tiles, blocks, brow, bcol, bcount, cell, gene):
    slots, width, _ = blocks.shape
    rank = gene.shape[-1]
    return pl.pallas_call(
        kernel,
        out_shape=jax.ShapeDtypeStruct((tiles, width, rank), F32),
        in_specs=[ANY, SMEM, SMEM, SMEM, VMEM, VMEM],
        out_specs=VMEM,
        scratch_shapes=[
            pltpu.VMEM((slots, width, width), BF),
            pltpu.VMEM((gene.shape[0], rank, width), BF),
            pltpu.SemaphoreType.DMA((slots,)),
        ],
        compiler_params=pltpu.CompilerParams(),
        name=name,
    )(blocks, brow, bcol, bcount, cell, gene)


def finish_kernel(cells, numer, gene, sums, fresh, other, other_sum, hold_sum, s1, r1, s2, r2):
    me = lax.axis_index("cell")
    barrier = pltpu.get_barrier_semaphore()
    for d in range(1, cells):
        pl.semaphore_signal(
            barrier, inc=1, device_id={"cell": lax.rem(me + d, cells)}, device_id_type=MESH
        )
    pl.semaphore_wait(barrier, cells - 1)
    tiles = numer.shape[0]
    sum_copies, copies = {}, {}
    for d in range(1, cells):
        where = {"cell": lax.rem(me + d, cells)}
        sum_copies[d] = send(sums, other_sum.at[d], s2.at[d], r2.at[d], where)
    for t in range(tiles):
        for d in range(1, cells):
            where = {"cell": lax.rem(me + d, cells)}
            copies[t, d] = send(numer.at[t], other.at[d, t], s1.at[d, t], r1.at[d, t], where)
    total = jnp.sum(sums[...], axis=0)
    for d in range(1, cells):
        sum_copies[d].wait()
        total += jnp.sum(other_sum[d], axis=0)
    for t in range(tiles):
        value = numer[t]
        for d in range(1, cells):
            copies[t, d].wait()
            value += other[d, t]
        fresh[t] = gene[t] * value / total


def finish(cells, numer, gene, sums):
    tiles, width, rank = numer.shape
    dma = pltpu.SemaphoreType.DMA
    return pl.pallas_call(
        functools.partial(finish_kernel, cells),
        out_shape=jax.ShapeDtypeStruct(numer.shape, F32),
        in_specs=[VMEM] * 3,
        out_specs=VMEM,
        scratch_shapes=[
            pltpu.VMEM((cells,) + numer.shape, F32),
            pltpu.VMEM((cells,) + sums.shape, F32),
            pltpu.VMEM((8, rank), F32),
            dma((cells, tiles)), dma((cells, tiles)), dma((cells,)), dma((cells,)),
        ],
        compiler_params=pltpu.CompilerParams(collective_id=2, has_side_effects=True),
        name="finish_genes",
    )(numer, gene.reshape(numer.shape), sums)


def on_device(cells, group, blocks, brow, bcol, bcount, cell_factor, gene_factor):
    width = blocks.shape[1]
    rows, rank = cell_factor.shape
    row_tiles = rows * group // width
    gene_bf = gene_factor.astype(BF).reshape(-1, width, rank)
    sums = jnp.sum(gene_factor, 0, keepdims=True)
    cell_bf, totals = gather(group, cell_factor.astype(BF), sums)
    cell_bf = cell_bf.reshape(row_tiles, width, rank)
    numer = block_pass(pass_one_kernel, "pass_one", row_tiles, blocks, brow, bcol, bcount,
                       cell_bf, gene_bf)
    cell_new, new_bf, parts = update_cells(group, numer, totals, cell_factor)
    new_bf = new_bf.reshape(row_tiles, width, rank)
    numer_gene = block_pass(pass_two_kernel, "pass_two", gene_bf.shape[0], blocks, brow, bcol,
                            bcount, new_bf, gene_bf)
    gene_new = finish(cells, numer_gene, gene_factor, parts)
    return cell_new, gene_new.reshape(gene_factor.shape)


def solution(mesh):
    sizes = dict(mesh.shape)
    placed = (
        P(("cell", "gene"), None, None),
        P(("cell", "gene")),
        P(("cell", "gene")),
        P(("cell", "gene")),
        P(("cell", "gene"), None),
        P("gene", None),
    )
    return jax.shard_map(
        functools.partial(on_device, sizes["cell"], sizes["gene"]),
        mesh=mesh,
        in_specs=placed,
        out_specs=(P(("cell", "gene"), None), P("gene", None)),
        check_vma=False,
    )
```

```python
import functools

import jax
import jax.numpy as jnp
from jax import lax
from jax.experimental import pallas as pl
from jax.experimental.pallas import tpu as pltpu
from jax.sharding import PartitionSpec as P

MESH = pl.DeviceIdType.MESH
F32 = jnp.float32
BF = jnp.bfloat16


def digits(group):
    cores = 2
    far = 4
    return far, group // (far * cores), cores


class Spot:
    def __init__(self, group):
        self.group = group
        self.far, self.near, self.cores = digits(group)
        self.me = lax.axis_index("gene")
        self.a = self.me // (self.near * self.cores)
        self.b = lax.rem(self.me // self.cores, self.near)
        self.c = lax.rem(self.me, self.cores)

    def a_at(self, d):
        return lax.rem(self.a + d, self.far)

    def b_at(self, d):
        return lax.rem(self.b + d, self.near)

    def index(self, a, b, c):
        return (a * self.near + b) * self.cores + c


def send(src, dst, send_sem, recv_sem, where):
    copy = pltpu.make_async_remote_copy(
        src_ref=src, dst_ref=dst, send_sem=send_sem, recv_sem=recv_sem,
        device_id=where, device_id_type=MESH,
    )
    copy.start()
    return copy


def greet(axis, size):
    barrier = pltpu.get_barrier_semaphore()
    me = lax.axis_index(axis)
    for d in range(1, size):
        pl.semaphore_signal(
            barrier, inc=1, device_id={axis: lax.rem(me + d, size)}, device_id_type=MESH
        )


def far_order(far):
    order = []
    for step in range(1, far // 2 + 1):
        order.append(step)
        if far - step != step:
            order.append(far - step)
    return order


class Gather:
    def __init__(self, spot, own, out, sems):
        self.spot, self.own, self.out = spot, own, out
        self.zs, self.zr, self.xs, self.xr, self.cs, self.cr = sems
        self.zc, self.xc, self.cc = {}, {}, {}

    def place(self, d, e):
        spot = self.spot
        return self.out.at[spot.index(spot.a_at(d), spot.b_at(e), spot.c)]

    def start(self, order):
        spot = self.spot
        for d in order:
            self.zc[d] = send(self.own, self.out.at[spot.me], self.zs.at[d], self.zr.at[d],
                              {"gene": spot.index(spot.a_at(spot.far - d), spot.b, spot.c)})
        self.forward(0, self.own)

    def forward(self, d, src):
        spot = self.spot
        for e in range(1, spot.near):
            self.xc[d, e] = send(src, self.place(d, 0), self.xs.at[d, e], self.xr.at[d, e],
                                 {"gene": spot.index(spot.a, spot.b_at(spot.near - e), spot.c)})
        self.pair(d, 0, src)

    def pair(self, d, e, src):
        spot = self.spot
        self.cc[d, e] = send(src, self.place(d, e), self.cs.at[d, e], self.cr.at[d, e],
                             {"gene": spot.index(spot.a, spot.b, 1 - spot.c)})

    def take_far(self, d):
        self.zc[d].wait_recv()
        self.forward(d, self.place(d, 0))

    def take_near(self, d):
        for e in range(1, self.spot.near):
            self.xc[d, e].wait_recv()
            self.pair(d, e, self.place(d, e))

    def ready(self, d):
        for e in range(self.spot.near):
            self.cc[d, e].wait_recv()

    def close(self):
        for copy in [*self.zc.values(), *self.xc.values(), *self.cc.values()]:
            copy.wait_send()


def gather_sems(far, near):
    dma = pltpu.SemaphoreType.DMA
    return [dma((far,))] * 2 + [dma((far, near))] * 4


def share(spot, src, parts, ss, sr):
    return [
        send(src, parts.at[spot.me], ss.at[d], sr.at[d], {"gene": lax.rem(spot.me + d, spot.group)})
        for d in range(1, spot.group)
    ]


def step_kernel(group, cells, blocks, table, cell, gene, cell_new, gene_new,
                held, gene_bf, flipped, own_bf, own_sum, parts, cell_bf,
                next_bf, next_sum, next_parts, next_cell, numer, p1, p2, p3, t2, t3,
                acc, other, group_sum, other_sum, *sems):
    spot = Spot(group)
    far, near = spot.far, spot.near
    a, b, c = spot.a, spot.b, spot.c
    slots, width, _ = blocks.shape
    tiles = gene.shape[0]
    rows = cell.shape[0]
    sub = width // rows
    one_sems, two_sems = sems[0:6], sems[6:12]
    s1, r1, s2, r2, s3, r3, gs, gr, ns, nr, fs, fr, os, orr, ls = sems[12:]
    load = pltpu.make_async_copy(blocks, held.at[pl.ds(0, slots)], ls.at[0])
    load.start()

    greet("gene", group)
    greet("cell", cells)
    held[slots] = jnp.zeros((width, width), BF)
    own_bf[...] = cell[...].astype(BF)
    cell_bf[spot.me] = cell[...].astype(BF)
    first_sum = jnp.zeros((1, gene.shape[-1]), F32)
    for j in range(tiles):
        first_sum += jnp.sum(gene[j], axis=0, keepdims=True)
    own_sum[...] = first_sum
    parts[spot.me] = first_sum
    pl.semaphore_wait(pltpu.get_barrier_semaphore(), group - 1 + cells - 1)

    order = far_order(far) + [0]
    one = Gather(spot, own_bf, cell_bf, one_sems)
    one.start(order[:-1])
    shared = share(spot, own_sum, parts, gs, gr)
    for j in range(tiles):
        gene_bf[j] = gene[j].astype(BF)
        flipped[j] = gene[j].astype(BF).T
    load.wait()
    for i, d in enumerate(order[:-1]):
        one.take_far(d)
        if i == 1:
            one.take_near(0)
            one.take_near(order[0])

    def ratio_of(source, g, j):
        rows_bf = source[g]
        slot = table[(g // sub) * tiles + j]
        if sub == 1:
            x = held[slot]
        else:
            x = held[slot, pl.ds(pl.multiple_of(lax.rem(g, sub) * rows, rows), rows), :]
        model = jnp.dot(rows_bf, flipped[j], preferred_element_type=F32)
        return (x.astype(F32) / model).astype(BF), rows_bf

    def first_half(d, core):
        def body(e, carry):
            g = spot.index(spot.a_at(d), spot.b_at(e), core)
            total = None
            for j in range(tiles):
                ratio, _ = ratio_of(cell_bf, g, j)
                term = jnp.dot(ratio, gene_bf[j], preferred_element_type=F32)
                total = term if total is None else total + term
            numer[g] = total
            return carry

        lax.fori_loop(0, near, body, 0)

    c1, c2, c3 = {}, {}, {}

    def stage_one(d):
        for e in [*range(1, near), 0]:
            at = spot.index(spot.a_at(d), spot.b_at(e), 1 - c)
            c1[d, e] = send(numer.at[at], p1.at[d, e], s1.at[d, e], r1.at[d, e],
                            {"gene": spot.index(a, b, 1 - c)})

    def stage_two(d):
        for e in range(1, near):
            c1[d, e].wait_recv()
            t2[d, e] = numer[spot.index(spot.a_at(d), spot.b_at(e), c)] + p1[d, e]
            c2[d, e] = send(t2.at[d, e], p2.at[d, e], s2.at[d, e], r2.at[d, e],
                            {"gene": spot.index(a, spot.b_at(e), c)})

    def summed(d):
        c1[d, 0].wait_recv()
        value = numer[spot.index(spot.a_at(d), b, c)] + p1[d, 0]
        for e in range(1, near):
            c2[d, e].wait_recv()
            value += p2[d, e]
        return value

    def stage_three(d):
        t3[d] = summed(d)
        c3[d] = send(t3.at[d], p3.at[d], s3.at[d], r3.at[d],
                     {"gene": spot.index(spot.a_at(d), b, c)})

    for i, d in enumerate(order):
        one.ready(d)
        first_half(d, 1 - c)
        stage_one(d)
        if i == 0:
            for other_d in order[1:-1]:
                one.take_near(other_d)
        if i >= 2:
            stage_three(order[i - 2])
        first_half(d, c)
        stage_two(d)
    stage_three(order[-2])
    for copy in shared:
        copy.wait()
    total = jnp.sum(parts[...], axis=0)
    value = summed(0)
    for d in order[:-1]:
        c3[d].wait_recv()
        value += p3[d]
    fresh = cell[...] * value / total
    next_bf[...] = fresh.astype(BF)
    next_cell[spot.me] = fresh.astype(BF)
    cell_new[...] = fresh
    fresh_sum = jnp.sum(fresh, axis=0, keepdims=True)
    next_sum[...] = fresh_sum
    next_parts[spot.me] = fresh_sum

    two = Gather(spot, next_bf, next_cell, two_sems)
    later = [d for d in range(1, far) if d != far // 2] + [far // 2]
    two.start(later)
    shared = share(spot, next_sum, next_parts, ns, nr)
    acc[...] = jnp.zeros_like(acc)

    def second_half(d, core, columns):
        def body(e, carry):
            g = spot.index(spot.a_at(d), spot.b_at(e), core)
            for j in columns:
                ratio, rows_bf = ratio_of(next_cell, g, j)
                acc[j] += lax.dot_general(
                    ratio, rows_bf, (((0,), (0,)), ((), ())), preferred_element_type=F32
                )
            return carry

        lax.fori_loop(0, near, body, 0)

    every = range(tiles)
    two.take_near(0)
    two.take_far(later[0])
    two.ready(0)
    second_half(0, c, every)
    two.take_far(later[1])
    second_half(0, 1 - c, every)
    two.take_far(later[2])
    two.take_near(later[0])
    two.take_near(later[1])
    second_half(later[0], c, every)
    two.take_near(later[2])
    two.ready(later[0])
    second_half(later[0], 1 - c, every)
    two.ready(later[1])
    two.ready(later[2])

    mine = lax.axis_index("cell")
    for copy in shared:
        copy.wait()
    sums = jnp.sum(next_parts[...], axis=0)
    group_sum[...] = sums
    sum_copies, copies = {}, {}
    for d in range(1, cells):
        sum_copies[d] = send(group_sum, other_sum.at[d], os.at[d], orr.at[d],
                             {"cell": lax.rem(mine + d, cells)})
    for j in every:
        for d in later[1:]:
            for core in (0, 1):
                second_half(d, core, [j])
        for d in range(1, cells):
            copies[j, d] = send(acc.at[j], other.at[d, j], fs.at[d, j], fr.at[d, j],
                                {"cell": lax.rem(mine + d, cells)})
    for d in range(1, cells):
        sum_copies[d].wait()
        sums += other_sum[d]
    for j in every:
        value = acc[j]
        for d in range(1, cells):
            copies[j, d].wait()
            value += other[d, j]
        gene_new[j] = gene[j] * value / sums
    one.close()
    two.close()
    for copy in [*c1.values(), *c2.values(), *c3.values()]:
        copy.wait_send()


VMEM = pl.BlockSpec(memory_space=pltpu.VMEM)
SMEM = pl.BlockSpec(memory_space=pltpu.SMEM)
ANY = pl.BlockSpec(memory_space=pl.ANY)


def step(group, cells, blocks, table, cell, gene):
    far, near, _ = digits(group)
    slots, width, _ = blocks.shape
    tiles, _, rank = gene.shape
    rows = cell.shape[0]
    dma = pltpu.SemaphoreType.DMA
    vmem = pltpu.VMEM
    return pl.pallas_call(
        functools.partial(step_kernel, group, cells),
        out_shape=(
            jax.ShapeDtypeStruct(cell.shape, F32),
            jax.ShapeDtypeStruct(gene.shape, F32),
        ),
        in_specs=[ANY, SMEM, VMEM, VMEM],
        out_specs=(VMEM, VMEM),
        scratch_shapes=[
            vmem((slots + 1, width, width), BF),
            vmem((tiles, width, rank), BF),
            vmem((tiles, rank, width), BF),
            vmem((rows, rank), BF),
            vmem((1, rank), F32),
            vmem((group, 1, rank), F32),
            vmem((group, rows, rank), BF),
            vmem((rows, rank), BF),
            vmem((1, rank), F32),
            vmem((group, 1, rank), F32),
            vmem((group, rows, rank), BF),
            vmem((group, rows, rank), F32),
            vmem((far, near, rows, rank), F32),
            vmem((far, near, rows, rank), F32),
            vmem((far, rows, rank), F32),
            vmem((far, near, rows, rank), F32),
            vmem((far, rows, rank), F32),
            vmem((tiles, width, rank), F32),
            vmem((cells, tiles, width, rank), F32),
            vmem((1, rank), F32),
            vmem((cells, 1, rank), F32),
        ] + gather_sems(far, near) * 2 + [dma((far, near))] * 4 + [dma((far,))] * 2
        + [dma((group,))] * 4 + [dma((cells, tiles))] * 2 + [dma((cells,))] * 2 + [dma((1,))],
        compiler_params=pltpu.CompilerParams(
            collective_id=0, has_side_effects=True, vmem_limit_bytes=60 * 1024 * 1024
        ),
        name="update_step",
    )(blocks, table, cell, gene)


def on_device(cells, group, blocks, brow, bcol, bcount, cell_factor, gene_factor):
    slots, width, _ = blocks.shape
    rows, rank = cell_factor.shape
    tiles = gene_factor.shape[0] // width
    spots = jnp.arange(rows * group // width * tiles, dtype=jnp.int32)
    order = jnp.arange(slots, dtype=jnp.int32)
    where = jnp.where(order < bcount[0], brow * tiles + bcol, -1)
    table = jnp.min(jnp.where(spots[:, None] == where[None, :], order[None, :], slots), axis=1)
    cell_new, gene_new = step(group, cells, blocks, table, cell_factor,
                              gene_factor.reshape(tiles, width, rank))
    return cell_new, gene_new.reshape(gene_factor.shape)


def solution(mesh):
    sizes = dict(mesh.shape)
    placed = (
        P(("cell", "gene"), None, None),
        P(("cell", "gene")),
        P(("cell", "gene")),
        P(("cell", "gene")),
        P(("cell", "gene"), None),
        P("gene", None),
    )
    return jax.shard_map(
        functools.partial(on_device, sizes["cell"], sizes["gene"]),
        mesh=mesh,
        in_specs=placed,
        out_specs=(P(("cell", "gene"), None), P("gene", None)),
        check_vma=False,
    )
```

```python
import functools

import jax
import jax.numpy as jnp
from jax import lax
from jax.experimental import pallas as pl
from jax.experimental.pallas import tpu as pltpu
from jax.sharding import PartitionSpec as P

MESH = pl.DeviceIdType.MESH
F32 = jnp.float32
BF = jnp.bfloat16
I16 = jnp.int16


def digits(group):
    cores = 2
    far = 4
    return far, group // (far * cores), cores


class Spot:
    def __init__(self, group):
        self.group = group
        self.far, self.near, self.cores = digits(group)
        self.me = lax.axis_index("gene")
        self.a = self.me // (self.near * self.cores)
        self.b = lax.rem(self.me // self.cores, self.near)
        self.c = lax.rem(self.me, self.cores)

    def a_at(self, d):
        return lax.rem(self.a + d, self.far)

    def b_at(self, d):
        return lax.rem(self.b + d, self.near)

    def index(self, a, b, c):
        return (a * self.near + b) * self.cores + c


def send(src, dst, send_sem, recv_sem, where):
    copy = pltpu.make_async_remote_copy(
        src_ref=src, dst_ref=dst, send_sem=send_sem, recv_sem=recv_sem,
        device_id=where, device_id_type=MESH,
    )
    copy.start()
    return copy


def greet(axis, size):
    barrier = pltpu.get_barrier_semaphore()
    me = lax.axis_index(axis)
    for d in range(1, size):
        pl.semaphore_signal(
            barrier, inc=1, device_id={axis: lax.rem(me + d, size)}, device_id_type=MESH
        )


def encode(value, code, scale):
    top = jnp.max(jnp.abs(value), axis=0, keepdims=True)
    factor = jnp.where(top > 0.0, 32767.0 / top, 0.0)
    code[...] = jnp.round(value * factor).astype(jnp.int32).astype(jnp.int16)
    scale[...] = top * (1.0 / 32767.0)


def decode(code, scale):
    return code[...].astype(jnp.int32).astype(F32) * scale[...]


def far_order(far):
    order = []
    for step in range(1, far // 2 + 1):
        order.append(step)
        if far - step != step:
            order.append(far - step)
    return order


class Gather:
    def __init__(self, spot, own, out, sems):
        self.spot, self.own, self.out = spot, own, out
        self.zs, self.zr, self.xs, self.xr, self.cs, self.cr = sems
        self.zc, self.xc, self.cc = {}, {}, {}

    def place(self, d, e):
        spot = self.spot
        return self.out.at[spot.index(spot.a_at(d), spot.b_at(e), spot.c)]

    def start(self, order):
        spot = self.spot
        for d in order:
            self.zc[d] = send(self.own, self.out.at[spot.me], self.zs.at[d], self.zr.at[d],
                              {"gene": spot.index(spot.a_at(spot.far - d), spot.b, spot.c)})
        self.forward(0, self.own)

    def forward(self, d, src):
        spot = self.spot
        for e in range(1, spot.near):
            self.xc[d, e] = send(src, self.place(d, 0), self.xs.at[d, e], self.xr.at[d, e],
                                 {"gene": spot.index(spot.a, spot.b_at(spot.near - e), spot.c)})
        self.pair(d, 0, src)

    def pair(self, d, e, src):
        spot = self.spot
        self.cc[d, e] = send(src, self.place(d, e), self.cs.at[d, e], self.cr.at[d, e],
                             {"gene": spot.index(spot.a, spot.b, 1 - spot.c)})

    def take_far(self, d):
        self.zc[d].wait_recv()
        self.forward(d, self.place(d, 0))

    def take_near(self, d):
        for e in range(1, self.spot.near):
            self.xc[d, e].wait_recv()
            self.pair(d, e, self.place(d, e))

    def ready(self, d):
        for e in range(self.spot.near):
            self.cc[d, e].wait_recv()

    def close(self):
        for copy in [*self.zc.values(), *self.xc.values(), *self.cc.values()]:
            copy.wait_send()


def gather_sems(far, near):
    dma = pltpu.SemaphoreType.DMA
    return [dma((far,))] * 2 + [dma((far, near))] * 4


def share(spot, src, parts, ss, sr):
    return [
        send(src, parts.at[spot.me], ss.at[d], sr.at[d], {"gene": lax.rem(spot.me + d, spot.group)})
        for d in range(1, spot.group)
    ]


def step_kernel(group, cells, blocks, table, cell, gene, cell_new, gene_new,
                held, gene_bf, flipped, own_bf, own_sum, parts, cell_bf,
                next_bf, next_sum, next_parts, next_cell, numer, p1, p2, p3, t2, t3,
                p2m, p3m, t2m, t3m, acc, code, codem, other, otherm, group_sum, other_sum, *sems):
    spot = Spot(group)
    far, near = spot.far, spot.near
    a, b, c = spot.a, spot.b, spot.c
    slots, width, _ = blocks.shape
    tiles = gene.shape[0]
    rows = cell.shape[0]
    sub = width // rows
    one_sems, two_sems = sems[0:6], sems[6:12]
    s1, r1, s2, r2, s3, r3, gs, gr, ns, nr, fs, fr, os, orr, ls, u2, v2, u3, v3, uf, vf = sems[12:]
    load = pltpu.make_async_copy(blocks, held.at[pl.ds(0, slots)], ls.at[0])
    load.start()

    greet("gene", group)
    greet("cell", cells)
    held[slots] = jnp.zeros((width, width), BF)
    own_bf[...] = cell[...].astype(BF)
    cell_bf[spot.me] = cell[...].astype(BF)
    first_sum = jnp.zeros((1, gene.shape[-1]), F32)
    for j in range(tiles):
        first_sum += jnp.sum(gene[j], axis=0, keepdims=True)
    own_sum[...] = first_sum
    parts[spot.me] = first_sum
    pl.semaphore_wait(pltpu.get_barrier_semaphore(), group - 1 + cells - 1)

    order = far_order(far) + [0]
    one = Gather(spot, own_bf, cell_bf, one_sems)
    one.start(order[:-1])
    shared = share(spot, own_sum, parts, gs, gr)
    for j in range(tiles):
        gene_bf[j] = gene[j].astype(BF)
        flipped[j] = gene[j].astype(BF).T
    load.wait()
    one.take_near(0)

    def ratio_of(source, g, j):
        rows_bf = source[g]
        slot = table[(g // sub) * tiles + j]
        if sub == 1:
            x = held[slot]
        else:
            x = held[slot, pl.ds(pl.multiple_of(lax.rem(g, sub) * rows, rows), rows), :]
        model = jnp.dot(rows_bf, flipped[j], preferred_element_type=F32)
        return (x.astype(F32) / model).astype(BF), rows_bf

    def first_half(d, core):
        def body(e, carry):
            g = spot.index(spot.a_at(d), spot.b_at(e), core)
            total = None
            for j in range(tiles):
                ratio, _ = ratio_of(cell_bf, g, j)
                term = jnp.dot(ratio, gene_bf[j], preferred_element_type=F32)
                total = term if total is None else total + term
            numer[g] = total
            return carry

        lax.fori_loop(0, near, body, 0)

    c1, c2, c3 = {}, {}, {}

    def stage_one(d):
        for e in [*range(1, near), 0]:
            at = spot.index(spot.a_at(d), spot.b_at(e), 1 - c)
            c1[d, e] = send(numer.at[at], p1.at[d, e], s1.at[d, e], r1.at[d, e],
                            {"gene": spot.index(a, b, 1 - c)})

    def weight(g):
        return jnp.mean(cell_bf[g].astype(F32), axis=1, keepdims=True)

    def stage_two(d):
        for e in range(1, near):
            c1[d, e].wait_recv()
            g = spot.index(spot.a_at(d), spot.b_at(e), c)
            encode((numer[g] + p1[d, e]) * weight(g), t2.at[d, e], t2m.at[d, e])
            where = {"gene": spot.index(a, spot.b_at(e), c)}
            c2[d, e] = (
                send(t2.at[d, e], p2.at[d, e], s2.at[d, e], r2.at[d, e], where),
                send(t2m.at[d, e], p2m.at[d, e], u2.at[d, e], v2.at[d, e], where),
            )

    def summed(d):
        c1[d, 0].wait_recv()
        g = spot.index(spot.a_at(d), b, c)
        value = (numer[g] + p1[d, 0]) * weight(g)
        for e in range(1, near):
            for copy in c2[d, e]:
                copy.wait_recv()
            value += decode(p2.at[d, e], p2m.at[d, e])
        return value

    def stage_three(d):
        encode(summed(d), t3.at[d], t3m.at[d])
        where = {"gene": spot.index(spot.a_at(d), b, c)}
        c3[d] = (
            send(t3.at[d], p3.at[d], s3.at[d], r3.at[d], where),
            send(t3m.at[d], p3m.at[d], u3.at[d], v3.at[d], where),
        )

    one.ready(0)
    first_half(0, 1 - c)
    stage_one(0)
    for i, d in enumerate(order[:-1]):
        one.take_far(d)
        if i == 0:
            continue
        one.take_near(order[i - 1])
    one.take_near(order[-2])
    for i, d in enumerate(order[:-1]):
        one.ready(d)
        first_half(d, 1 - c)
        stage_one(d)
        if i >= 2:
            stage_three(order[i - 2])
        first_half(d, c)
        stage_two(d)
    stage_three(order[-3])
    first_half(0, c)
    stage_two(0)
    stage_three(order[-2])
    for copy in shared:
        copy.wait()
    total = jnp.sum(parts[...], axis=0)
    value = summed(0)
    for d in order[:-1]:
        for copy in c3[d]:
            copy.wait_recv()
        value += decode(p3.at[d], p3m.at[d])
    fresh = cell[...] * (value / weight(spot.me)) / total
    next_bf[...] = fresh.astype(BF)
    next_cell[spot.me] = fresh.astype(BF)
    cell_new[...] = fresh
    fresh_sum = jnp.sum(fresh, axis=0, keepdims=True)
    next_sum[...] = fresh_sum
    next_parts[spot.me] = fresh_sum

    two = Gather(spot, next_bf, next_cell, two_sems)
    later = [d for d in range(1, far) if d != far // 2] + [far // 2]
    two.start(later)
    shared = share(spot, next_sum, next_parts, ns, nr)
    acc[...] = jnp.zeros_like(acc)

    def second_half(d, core, columns):
        def body(e, carry):
            g = spot.index(spot.a_at(d), spot.b_at(e), core)
            for j in columns:
                ratio, rows_bf = ratio_of(next_cell, g, j)
                acc[j] += lax.dot_general(
                    ratio, rows_bf, (((0,), (0,)), ((), ())), preferred_element_type=F32
                )
            return carry

        lax.fori_loop(0, near, body, 0)

    every = range(tiles)
    two.take_near(0)
    two.take_far(later[0])
    two.ready(0)
    second_half(0, c, every)
    two.take_far(later[1])
    second_half(0, 1 - c, every)
    two.take_far(later[2])
    two.take_near(later[0])
    two.take_near(later[1])
    second_half(later[0], c, every)
    two.take_near(later[2])
    two.ready(later[0])
    second_half(later[0], 1 - c, every)
    two.ready(later[1])
    two.ready(later[2])

    mine = lax.axis_index("cell")
    for copy in shared:
        copy.wait()
    sums = jnp.sum(next_parts[...], axis=0)
    group_sum[...] = sums
    other_sum[mine] = sums
    sum_copies, copies = {}, {}
    for d in range(1, cells):
        sum_copies[d] = send(group_sum, other_sum.at[mine], os.at[d], orr.at[d],
                             {"cell": lax.rem(mine + d, cells)})

    def balance(j):
        return jnp.mean(gene_bf[j].astype(F32), axis=1, keepdims=True)

    for j in every:
        for d in later[1:]:
            for core in (0, 1):
                second_half(d, core, [j])
        encode(acc[j] * balance(j), code.at[j], codem.at[j])
        other[mine, j] = code[j]
        otherm[mine, j] = codem[j]
        for d in range(1, cells):
            where = {"cell": lax.rem(mine + d, cells)}
            copies[j, d] = (
                send(code.at[j], other.at[mine, j], fs.at[d, j], fr.at[d, j], where),
                send(codem.at[j], otherm.at[mine, j], uf.at[d, j], vf.at[d, j], where),
            )
    for d in range(1, cells):
        sum_copies[d].wait()
    sums = other_sum[0]
    for k in range(1, cells):
        sums += other_sum[k]
    for j in every:
        for d in range(1, cells):
            for copy in copies[j, d]:
                copy.wait()
        value = decode(other.at[0, j], otherm.at[0, j])
        for k in range(1, cells):
            value += decode(other.at[k, j], otherm.at[k, j])
        gene_new[j] = gene[j] * (value / balance(j)) / sums
    one.close()
    two.close()
    for copy in c1.values():
        copy.wait_send()
    for pair in [*c2.values(), *c3.values()]:
        for copy in pair:
            copy.wait_send()


VMEM = pl.BlockSpec(memory_space=pltpu.VMEM)
SMEM = pl.BlockSpec(memory_space=pltpu.SMEM)
ANY = pl.BlockSpec(memory_space=pl.ANY)


def step(group, cells, blocks, table, cell, gene):
    far, near, _ = digits(group)
    slots, width, _ = blocks.shape
    tiles, _, rank = gene.shape
    rows = cell.shape[0]
    dma = pltpu.SemaphoreType.DMA
    vmem = pltpu.VMEM
    return pl.pallas_call(
        functools.partial(step_kernel, group, cells),
        out_shape=(
            jax.ShapeDtypeStruct(cell.shape, F32),
            jax.ShapeDtypeStruct(gene.shape, F32),
        ),
        in_specs=[ANY, SMEM, VMEM, VMEM],
        out_specs=(VMEM, VMEM),
        scratch_shapes=[
            vmem((slots + 1, width, width), BF),
            vmem((tiles, width, rank), BF),
            vmem((tiles, rank, width), BF),
            vmem((rows, rank), BF),
            vmem((1, rank), F32),
            vmem((group, 1, rank), F32),
            vmem((group, rows, rank), BF),
            vmem((rows, rank), BF),
            vmem((1, rank), F32),
            vmem((group, 1, rank), F32),
            vmem((group, rows, rank), BF),
            vmem((group, rows, rank), F32),
            vmem((far, near, rows, rank), F32),
            vmem((far, near, rows, rank), I16),
            vmem((far, rows, rank), I16),
            vmem((far, near, rows, rank), I16),
            vmem((far, rows, rank), I16),
            vmem((far, near, 1, rank), F32),
            vmem((far, 1, rank), F32),
            vmem((far, near, 1, rank), F32),
            vmem((far, 1, rank), F32),
            vmem((tiles, width, rank), F32),
            vmem((tiles, width, rank), I16),
            vmem((tiles, 1, rank), F32),
            vmem((cells, tiles, width, rank), I16),
            vmem((cells, tiles, 1, rank), F32),
            vmem((1, rank), F32),
            vmem((cells, 1, rank), F32),
        ] + gather_sems(far, near) * 2 + [dma((far, near))] * 4 + [dma((far,))] * 2
        + [dma((group,))] * 4 + [dma((cells, tiles))] * 2 + [dma((cells,))] * 2 + [dma((1,))]
        + [dma((far, near))] * 2 + [dma((far,))] * 2 + [dma((cells, tiles))] * 2,
        compiler_params=pltpu.CompilerParams(
            collective_id=0, has_side_effects=True, vmem_limit_bytes=60 * 1024 * 1024
        ),
        name="update_step",
    )(blocks, table, cell, gene)


def on_device(cells, group, blocks, brow, bcol, bcount, cell_factor, gene_factor):
    slots, width, _ = blocks.shape
    rows, rank = cell_factor.shape
    tiles = gene_factor.shape[0] // width
    spots = jnp.arange(rows * group // width * tiles, dtype=jnp.int32)
    order = jnp.arange(slots, dtype=jnp.int32)
    where = jnp.where(order < bcount[0], brow * tiles + bcol, -1)
    table = jnp.min(jnp.where(spots[:, None] == where[None, :], order[None, :], slots), axis=1)
    cell_new, gene_new = step(group, cells, blocks, table, cell_factor,
                              gene_factor.reshape(tiles, width, rank))
    return cell_new, gene_new.reshape(gene_factor.shape)


def solution(mesh):
    sizes = dict(mesh.shape)
    placed = (
        P(("cell", "gene"), None, None),
        P(("cell", "gene")),
        P(("cell", "gene")),
        P(("cell", "gene")),
        P(("cell", "gene"), None),
        P("gene", None),
    )
    return jax.shard_map(
        functools.partial(on_device, sizes["cell"], sizes["gene"]),
        mesh=mesh,
        in_specs=placed,
        out_specs=(P(("cell", "gene"), None), P("gene", None)),
        check_vma=False,
    )
```

```python
import functools

import jax
import jax.numpy as jnp
from jax import lax
from jax.experimental import pallas as pl
from jax.experimental.pallas import tpu as pltpu
from jax.sharding import PartitionSpec as P

MESH = pl.DeviceIdType.MESH
F32 = jnp.float32
BF = jnp.bfloat16
I16 = jnp.int16


def digits(group):
    cores = 2
    far = 4
    return far, group // (far * cores), cores


class Spot:
    def __init__(self, group):
        self.group = group
        self.far, self.near, self.cores = digits(group)
        self.me = lax.axis_index("gene")
        self.a = self.me // (self.near * self.cores)
        self.b = lax.rem(self.me // self.cores, self.near)
        self.c = lax.rem(self.me, self.cores)

    def a_at(self, d):
        return lax.rem(self.a + d, self.far)

    def b_at(self, d):
        return lax.rem(self.b + d, self.near)

    def index(self, a, b, c):
        return (a * self.near + b) * self.cores + c


def send(src, dst, send_sem, recv_sem, where):
    copy = pltpu.make_async_remote_copy(
        src_ref=src, dst_ref=dst, send_sem=send_sem, recv_sem=recv_sem,
        device_id=where, device_id_type=MESH,
    )
    copy.start()
    return copy


def greet(axis, size):
    barrier = pltpu.get_barrier_semaphore()
    me = lax.axis_index(axis)
    for d in range(1, size):
        pl.semaphore_signal(
            barrier, inc=1, device_id={axis: lax.rem(me + d, size)}, device_id_type=MESH
        )


def encode(value, code, scale):
    top = jnp.max(jnp.abs(value), axis=0, keepdims=True)
    factor = jnp.where(top > 0.0, 32767.0 / top, 0.0)
    code[...] = jnp.round(value * factor).astype(jnp.int32).astype(jnp.int16)
    scale[...] = top * (1.0 / 32767.0)


def decode(code, scale):
    return code[...].astype(jnp.int32).astype(F32) * scale[...]


def far_order(far):
    order = []
    for step in range(1, far // 2 + 1):
        order.append(step)
        if far - step != step:
            order.append(far - step)
    return order


class Gather:
    def __init__(self, spot, own, out, sems):
        self.spot, self.own, self.out = spot, own, out
        self.zs, self.zr, self.xs, self.xr, self.cs, self.cr = sems
        self.zc, self.xc, self.cc = {}, {}, {}

    def place(self, d, e):
        spot = self.spot
        return self.out.at[spot.index(spot.a_at(d), spot.b_at(e), spot.c)]

    def start(self, order):
        spot = self.spot
        for d in order:
            self.zc[d] = send(self.own, self.out.at[spot.me], self.zs.at[d], self.zr.at[d],
                              {"gene": spot.index(spot.a_at(spot.far - d), spot.b, spot.c)})
        self.forward(0, self.own)

    def forward(self, d, src):
        spot = self.spot
        for e in range(1, spot.near):
            self.xc[d, e] = send(src, self.place(d, 0), self.xs.at[d, e], self.xr.at[d, e],
                                 {"gene": spot.index(spot.a, spot.b_at(spot.near - e), spot.c)})
        self.pair(d, 0, src)

    def pair(self, d, e, src):
        spot = self.spot
        self.cc[d, e] = send(src, self.place(d, e), self.cs.at[d, e], self.cr.at[d, e],
                             {"gene": spot.index(spot.a, spot.b, 1 - spot.c)})

    def take_far(self, d):
        self.zc[d].wait_recv()
        self.forward(d, self.place(d, 0))

    def take_near(self, d):
        for e in range(1, self.spot.near):
            self.xc[d, e].wait_recv()
            self.pair(d, e, self.place(d, e))

    def ready(self, d):
        for e in range(self.spot.near):
            self.cc[d, e].wait_recv()

    def close(self):
        for copy in [*self.zc.values(), *self.xc.values(), *self.cc.values()]:
            copy.wait_send()


def gather_sems(far, near):
    dma = pltpu.SemaphoreType.DMA
    return [dma((far,))] * 2 + [dma((far, near))] * 4


def share(spot, src, parts, ss, sr):
    return [
        send(src, parts.at[spot.me], ss.at[d], sr.at[d], {"gene": lax.rem(spot.me + d, spot.group)})
        for d in range(1, spot.group)
    ]


def step_kernel(group, cells, blocks, table, cell, gene, cell_new, gene_new,
                held, gene_bf, flipped, own_bf, own_sum, parts, cell_bf,
                next_bf, next_sum, next_parts, next_cell, numer, p1, p2, p3, t2, t3,
                p2m, p3m, t2m, t3m, acc, code, codem, other, otherm, group_sum, other_sum, *sems):
    spot = Spot(group)
    far, near = spot.far, spot.near
    a, b, c = spot.a, spot.b, spot.c
    slots, width, _ = blocks.shape
    tiles = gene.shape[0]
    rows = cell.shape[0]
    sub = width // rows
    one_sems, two_sems = sems[0:6], sems[6:12]
    s1, r1, s2, r2, s3, r3, gs, gr, ns, nr, fs, fr, os, orr, ls, u2, v2, u3, v3, uf, vf = sems[12:]
    load = pltpu.make_async_copy(blocks, held.at[pl.ds(0, slots)], ls.at[0])
    load.start()

    greet("gene", group)
    greet("cell", cells)
    held[slots] = jnp.zeros((width, width), BF)
    own_bf[...] = cell[...].astype(BF)
    cell_bf[spot.me] = cell[...].astype(BF)
    pl.semaphore_wait(pltpu.get_barrier_semaphore(), group - 1 + cells - 1)

    order = far_order(far) + [0]
    one = Gather(spot, own_bf, cell_bf, one_sems)
    one.start(order[:-1])
    first_sum = jnp.zeros((1, gene.shape[-1]), F32)
    for j in range(tiles):
        first_sum += jnp.sum(gene[j], axis=0, keepdims=True)
    own_sum[...] = first_sum
    parts[spot.me] = first_sum
    shared = share(spot, own_sum, parts, gs, gr)
    for j in range(tiles):
        gene_bf[j] = gene[j].astype(BF)
        flipped[j] = gene[j].astype(BF).T
    one.take_near(0)
    load.wait()

    def ratio_of(source, g, j):
        rows_bf = source[g]
        slot = table[(g // sub) * tiles + j]
        if sub == 1:
            x = held[slot]
        else:
            x = held[slot, pl.ds(pl.multiple_of(lax.rem(g, sub) * rows, rows), rows), :]
        model = jnp.dot(rows_bf, flipped[j], preferred_element_type=F32)
        return (x.astype(F32) / model).astype(BF), rows_bf

    def first_half(d, core):
        def body(e, carry):
            g = spot.index(spot.a_at(d), spot.b_at(e), core)
            total = None
            for j in range(tiles):
                ratio, _ = ratio_of(cell_bf, g, j)
                term = jnp.dot(ratio, gene_bf[j], preferred_element_type=F32)
                total = term if total is None else total + term
            numer[g] = total
            return carry

        lax.fori_loop(0, near, body, 0)

    c1, c2, c3 = {}, {}, {}

    def stage_one(d):
        for e in [*range(1, near), 0]:
            at = spot.index(spot.a_at(d), spot.b_at(e), 1 - c)
            c1[d, e] = send(numer.at[at], p1.at[d, e], s1.at[d, e], r1.at[d, e],
                            {"gene": spot.index(a, b, 1 - c)})

    def weight(g):
        return jnp.mean(cell_bf[g].astype(F32), axis=1, keepdims=True)

    def stage_two(d):
        for e in range(1, near):
            c1[d, e].wait_recv()
            g = spot.index(spot.a_at(d), spot.b_at(e), c)
            encode((numer[g] + p1[d, e]) * weight(g), t2.at[d, e], t2m.at[d, e])
            where = {"gene": spot.index(a, spot.b_at(e), c)}
            c2[d, e] = (
                send(t2.at[d, e], p2.at[d, e], s2.at[d, e], r2.at[d, e], where),
                send(t2m.at[d, e], p2m.at[d, e], u2.at[d, e], v2.at[d, e], where),
            )

    def summed(d):
        c1[d, 0].wait_recv()
        g = spot.index(spot.a_at(d), b, c)
        value = (numer[g] + p1[d, 0]) * weight(g)
        for e in range(1, near):
            for copy in c2[d, e]:
                copy.wait_recv()
            value += decode(p2.at[d, e], p2m.at[d, e])
        return value

    def stage_three(d):
        encode(summed(d), t3.at[d], t3m.at[d])
        where = {"gene": spot.index(spot.a_at(d), b, c)}
        c3[d] = (
            send(t3.at[d], p3.at[d], s3.at[d], r3.at[d], where),
            send(t3m.at[d], p3m.at[d], u3.at[d], v3.at[d], where),
        )

    one.ready(0)
    first_half(0, 1 - c)
    stage_one(0)
    for i, d in enumerate(order[:-1]):
        one.take_far(d)
        if i == 0:
            continue
        one.take_near(order[i - 1])
    one.take_near(order[-2])
    for i, d in enumerate(order[:-1]):
        one.ready(d)
        first_half(d, 1 - c)
        stage_one(d)
        if i >= 2:
            stage_three(order[i - 2])
        first_half(d, c)
        stage_two(d)
    stage_three(order[-3])
    first_half(0, c)
    stage_two(0)
    stage_three(order[-2])
    for copy in shared:
        copy.wait()
    total = jnp.sum(parts[...], axis=0)
    value = summed(0)
    for d in order[:-1]:
        for copy in c3[d]:
            copy.wait_recv()
        value += decode(p3.at[d], p3m.at[d])
    fresh = cell[...] * (value / weight(spot.me)) / total
    next_bf[...] = fresh.astype(BF)
    next_cell[spot.me] = fresh.astype(BF)
    cell_new[...] = fresh
    fresh_sum = jnp.sum(fresh, axis=0, keepdims=True)
    next_sum[...] = fresh_sum
    next_parts[spot.me] = fresh_sum

    two = Gather(spot, next_bf, next_cell, two_sems)
    later = [d for d in range(1, far) if d != far // 2] + [far // 2]
    two.start(later)
    shared = share(spot, next_sum, next_parts, ns, nr)
    acc[...] = jnp.zeros_like(acc)

    def second_terms(chunks, j):
        total = None
        for g in chunks:
            ratio, rows_bf = ratio_of(next_cell, g, j)
            term = lax.dot_general(
                ratio, rows_bf, (((0,), (0,)), ((), ())), preferred_element_type=F32
            )
            total = term if total is None else total + term
        acc[j] += total

    def second_chunks(d, core, first, last):
        def body(e, carry):
            for j in every:
                second_terms([spot.index(spot.a_at(d), spot.b_at(e), core)], j)
            return carry

        lax.fori_loop(first, last, body, 0)

    def second_column(offsets, j):
        def body(e, carry):
            second_terms([spot.index(spot.a_at(d), spot.b_at(e), core)
                          for d in offsets for core in (0, 1)], j)
            return carry

        lax.fori_loop(0, near, body, 0)

    every = range(tiles)
    second_chunks(0, c, 0, 1)
    two.take_near(0)
    second_chunks(0, c, 1, near)
    two.ready(0)
    second_chunks(0, 1 - c, 0, near)
    for d in later:
        two.take_far(d)
    two.take_near(later[0])
    two.take_near(later[1])
    two.ready(later[0])
    second_chunks(later[0], c, 0, near)
    two.take_near(later[2])
    second_chunks(later[0], 1 - c, 0, near)
    two.ready(later[1])
    two.ready(later[2])

    mine = lax.axis_index("cell")
    for copy in shared:
        copy.wait()
    sums = jnp.sum(next_parts[...], axis=0)
    group_sum[...] = sums
    other_sum[mine] = sums
    sum_copies, copies = {}, {}
    for d in range(1, cells):
        sum_copies[d] = send(group_sum, other_sum.at[mine], os.at[d], orr.at[d],
                             {"cell": lax.rem(mine + d, cells)})

    def balance(j):
        return jnp.mean(gene_bf[j].astype(F32), axis=1, keepdims=True)

    for j in every:
        second_column(later[1:], j)
        encode(acc[j] * balance(j), code.at[j], codem.at[j])
        other[mine, j] = code[j]
        otherm[mine, j] = codem[j]
        for d in range(1, cells):
            where = {"cell": lax.rem(mine + d, cells)}
            copies[j, d] = (
                send(code.at[j], other.at[mine, j], fs.at[d, j], fr.at[d, j], where),
                send(codem.at[j], otherm.at[mine, j], uf.at[d, j], vf.at[d, j], where),
            )
    for d in range(1, cells):
        sum_copies[d].wait()
    sums = other_sum[0]
    for k in range(1, cells):
        sums += other_sum[k]
    for j in every:
        for d in range(1, cells):
            for copy in copies[j, d]:
                copy.wait()
        value = decode(other.at[0, j], otherm.at[0, j])
        for k in range(1, cells):
            value += decode(other.at[k, j], otherm.at[k, j])
        gene_new[j] = gene[j] * (value / balance(j)) / sums
    one.close()
    two.close()
    for copy in c1.values():
        copy.wait_send()
    for pair in [*c2.values(), *c3.values()]:
        for copy in pair:
            copy.wait_send()


VMEM = pl.BlockSpec(memory_space=pltpu.VMEM)
SMEM = pl.BlockSpec(memory_space=pltpu.SMEM)
ANY = pl.BlockSpec(memory_space=pl.ANY)


def step(group, cells, blocks, table, cell, gene):
    far, near, _ = digits(group)
    slots, width, _ = blocks.shape
    tiles, _, rank = gene.shape
    rows = cell.shape[0]
    dma = pltpu.SemaphoreType.DMA
    vmem = pltpu.VMEM
    return pl.pallas_call(
        functools.partial(step_kernel, group, cells),
        out_shape=(
            jax.ShapeDtypeStruct(cell.shape, F32),
            jax.ShapeDtypeStruct(gene.shape, F32),
        ),
        in_specs=[ANY, SMEM, VMEM, VMEM],
        out_specs=(VMEM, VMEM),
        scratch_shapes=[
            vmem((slots + 1, width, width), BF),
            vmem((tiles, width, rank), BF),
            vmem((tiles, rank, width), BF),
            vmem((rows, rank), BF),
            vmem((1, rank), F32),
            vmem((group, 1, rank), F32),
            vmem((group, rows, rank), BF),
            vmem((rows, rank), BF),
            vmem((1, rank), F32),
            vmem((group, 1, rank), F32),
            vmem((group, rows, rank), BF),
            vmem((group, rows, rank), F32),
            vmem((far, near, rows, rank), F32),
            vmem((far, near, rows, rank), I16),
            vmem((far, rows, rank), I16),
            vmem((far, near, rows, rank), I16),
            vmem((far, rows, rank), I16),
            vmem((far, near, 1, rank), F32),
            vmem((far, 1, rank), F32),
            vmem((far, near, 1, rank), F32),
            vmem((far, 1, rank), F32),
            vmem((tiles, width, rank), F32),
            vmem((tiles, width, rank), I16),
            vmem((tiles, 1, rank), F32),
            vmem((cells, tiles, width, rank), I16),
            vmem((cells, tiles, 1, rank), F32),
            vmem((1, rank), F32),
            vmem((cells, 1, rank), F32),
        ] + gather_sems(far, near) * 2 + [dma((far, near))] * 4 + [dma((far,))] * 2
        + [dma((group,))] * 4 + [dma((cells, tiles))] * 2 + [dma((cells,))] * 2 + [dma((1,))]
        + [dma((far, near))] * 2 + [dma((far,))] * 2 + [dma((cells, tiles))] * 2,
        compiler_params=pltpu.CompilerParams(
            collective_id=0, has_side_effects=True, vmem_limit_bytes=60 * 1024 * 1024
        ),
        name="update_step",
    )(blocks, table, cell, gene)


def on_device(cells, group, blocks, brow, bcol, bcount, cell_factor, gene_factor):
    slots, width, _ = blocks.shape
    rows, rank = cell_factor.shape
    tiles = gene_factor.shape[0] // width
    spots = jnp.arange(rows * group // width * tiles, dtype=jnp.int32)
    order = jnp.arange(slots, dtype=jnp.int32)
    where = jnp.where(order < bcount[0], brow * tiles + bcol, -1)
    table = jnp.min(jnp.where(spots[:, None] == where[None, :], order[None, :], slots), axis=1)
    cell_new, gene_new = step(group, cells, blocks, table, cell_factor,
                              gene_factor.reshape(tiles, width, rank))
    return cell_new, gene_new.reshape(gene_factor.shape)


def solution(mesh):
    sizes = dict(mesh.shape)
    placed = (
        P(("cell", "gene"), None, None),
        P(("cell", "gene")),
        P(("cell", "gene")),
        P(("cell", "gene")),
        P(("cell", "gene"), None),
        P("gene", None),
    )
    return jax.shard_map(
        functools.partial(on_device, sizes["cell"], sizes["gene"]),
        mesh=mesh,
        in_specs=placed,
        out_specs=(P(("cell", "gene"), None), P("gene", None)),
        check_vma=False,
    )
```
